32 devices in a mesh: group: 2 (over x), blk: 16 (over z, y, core).
Axes of the slice: x: 2, y: 2, z: 4, core: 2. Of those that a mesh axis runs over, the one named last changes fastest.
Arguments:
- queries: bfloat16 [4, 64, 2048], P('group', 'blk'), parts along dimension 0, may hold values from -160 to 160
- keys: bfloat16 [4, 20480, 256], P('group', 'blk'), parts along dimension 0, may hold values from -4 to 4
- values: bfloat16 [4, 20480, 256], P('group', 'blk'), parts along dimension 0, may hold values from -6 to 6
- lengths: int32 [4], P('group'), parts along dimension 0, may hold values from 15360 to 20480
- offsets: int32 [4], P('group'), parts along dimension 0, may hold values from 12800 to 20416
Outputs:
- attended: bfloat16 [4, 64, 2048], P('group', 'blk'), parts along dimension 0
The draws below stay inside these ranges and needn't reach their ends.
There are 2 independent parts, one for each index of `group`. The reference program is written for one: setup_inputs(seed, part) draws one part's arguments, and reference() takes and returns one part's arrays. A program takes and returns all parts, laid end to end along the dimension named above; each array names one. Nothing has to cross between parts.
All inputs are finite; a program needn't handle non-finite values.
Results may differ from the reference program's by a relative error of at most 0.0085.
Values may be sent and summed in bfloat16 or wider, within the bound.
No kernel may reach another device: no remote copies, remote signals or barrier semaphores. Data moves between devices by JAX's collectives and lax.ppermute only.
A program may use at most 64 MiB of HBM per device.

```python
import math
import jax
import jax.numpy as jnp
from jax import lax

HEADS = 16
KV_HEADS = 2
HEAD_DIM = 128
MICRO = 2
KEYS_DEV = 1280
QUERIES = 64
CONTEXT = 20480
N_BLK = 16


def draw_keys(key, part):
    array_shape = (MICRO, CONTEXT, KV_HEADS * HEAD_DIM)
    sampled = jnp.clip(jax.random.normal(jax.random.fold_in(key, 11), array_shape, jnp.float32), -4.0, 4.0)
    return sampled.astype(jnp.bfloat16)


def draw_queries(key, part):
    array_shape = (MICRO, QUERIES, HEADS * HEAD_DIM)
    sampled = jnp.clip(3.0 * jax.random.normal(jax.random.fold_in(key, 13), array_shape, jnp.float32), -12.0, 12.0)
    return sampled.astype(jnp.bfloat16)


def block_levels(rng, shape, pieces, least, top_value):
    gain, own = 1.0, jax.random.fold_in(rng, 6)
    for dim, shards_of in pieces:
        heights = jnp.exp(jax.random.uniform(jax.random.fold_in(own, dim), (shards_of,), jnp.float32, least / len(pieces), top_value / len(pieces)))
        gain = gain * jnp.repeat(heights, shape[dim] // shards_of).reshape([-1 if axis == dim else 1 for axis in range(len(shape))])
    return gain


def noise(key, dims, spread, most, split=(), kind=jnp.bfloat16):
    factor_of = block_levels(key, dims, split, -0.22, 0.18) if split else 1.0
    drawn = jax.random.normal(key, dims, jnp.float32) * spread * factor_of
    return jnp.minimum(jnp.maximum(drawn, -most), most).astype(kind)


def setup_inputs(seed: int = 0, part: int = 0) -> dict:
    streams_of = jax.random.split(jax.random.key(seed), 6)
    part_splits = jax.random.split(jax.random.fold_in(streams_of[5], part), 6)
    queries = draw_queries(jax.random.fold_in(jax.random.fold_in(streams_of[5], part), 71), part)
    keys = draw_keys(jax.random.fold_in(jax.random.fold_in(streams_of[5], part), 71), part)
    values = noise(part_splits[2], (MICRO, CONTEXT, KV_HEADS * HEAD_DIM), 1.0, 6.0, ((1, 16),))
    lengths = jax.random.randint(part_splits[3], (MICRO,), CONTEXT * 3 // 4, CONTEXT + 1).astype(jnp.int32)
    offsets = jax.random.randint(part_splits[4], (MICRO,), CONTEXT * 5 // 8, CONTEXT - QUERIES + 1).astype(jnp.int32)
    return {"queries": queries, "keys": keys, "values": values, "lengths": lengths, "offsets": offsets}


masked_low = -1e+30

def shard_partial(query_rows, key_rows, value_rows, query_pos, key_pos, lengths):
    micro_count, rows_count, row_width = query_rows.shape
    heads_count = row_width // HEAD_DIM
    group_size = heads_count // KV_HEADS
    query_split = query_rows.astype(jnp.float32).reshape(micro_count, rows_count, KV_HEADS, group_size, HEAD_DIM)
    key_split = key_rows.astype(jnp.float32).reshape(micro_count, key_rows.shape[1], KV_HEADS, HEAD_DIM)
    value_split = value_rows.astype(jnp.float32).reshape(micro_count, value_rows.shape[1], KV_HEADS, HEAD_DIM)
    scores = jnp.einsum('brkgd,bskd->bkgrs', query_split, key_split)
    scores = scores * (1.0 / math.sqrt(HEAD_DIM))
    visible = (key_pos[None, None, :] <= query_pos[:, :, None]) & (key_pos[None, None, :] < lengths[:, None, None])
    visible = visible[:, None, None, :, :]
    any_visible = jnp.any(visible, axis=-1)
    row_max = lax.optimization_barrier(jnp.max(jnp.where(visible, scores, masked_low), axis=-1))
    safe_max = jnp.where(any_visible, row_max, 0.0)
    shifted = jnp.where(visible, scores - safe_max[..., None], 0.0)
    weights = jnp.where(visible, jnp.exp(shifted), 0.0)
    totals = lax.optimization_barrier(jnp.sum(weights, axis=-1))
    bounded = jnp.maximum(totals, 1.0)
    rounded = lax.optimization_barrier(weights.astype(jnp.bfloat16)).astype(jnp.float32)
    numerator = jnp.einsum('bkgrs,bskd->bkgrd', rounded, value_split)
    partial_value = (numerator / bounded[..., None]).astype(jnp.bfloat16)
    partial_value = jnp.transpose(partial_value, (0, 3, 1, 2, 4)).reshape(micro_count, rows_count, row_width)
    logsum = jnp.where(any_visible, safe_max + jnp.log(bounded), masked_low)
    logsum = jnp.transpose(logsum, (0, 3, 1, 2)).reshape(micro_count, rows_count, heads_count)
    return (partial_value, logsum)

def reference(queries, keys, values, lengths, offsets):
    micro_count, all_rows, row_width = queries.shape
    heads_count = row_width // HEAD_DIM
    query_pos = offsets[:, None] + jnp.arange(all_rows, dtype=jnp.int32)[None, :]

    def visit(state, shard_index):
        best_log, scale_total, accumulated = state
        start_key = (shard_index * KEYS_DEV).astype(jnp.int32)
        key_rows = lax.dynamic_slice_in_dim(keys, start_key, KEYS_DEV, 1)
        value_rows = lax.dynamic_slice_in_dim(values, start_key, KEYS_DEV, 1)
        key_pos = start_key + jnp.arange(KEYS_DEV, dtype=jnp.int32)
        partial_value, logsum = shard_partial(queries, key_rows, value_rows, query_pos, key_pos, lengths)
        partial_value = lax.optimization_barrier(partial_value).astype(jnp.float32)
        partial_value = partial_value.reshape(micro_count, all_rows, heads_count, HEAD_DIM)
        newest = jnp.maximum(best_log, logsum)
        keep_old = jnp.exp(best_log - newest)
        take_new = jnp.exp(logsum - newest)
        new_total = scale_total * keep_old + take_new
        new_accum = accumulated * keep_old[..., None] + partial_value * take_new[..., None]
        return ((newest, new_total, new_accum), None)
    initial = (jnp.full((micro_count, all_rows, heads_count), masked_low, jnp.float32), jnp.zeros((micro_count, all_rows, heads_count), jnp.float32), jnp.zeros((micro_count, all_rows, heads_count, HEAD_DIM), jnp.float32))
    final_state, unused = lax.scan(visit, initial, jnp.arange(N_BLK, dtype=jnp.int32))
    best_log, scale_total, accumulated = final_state
    merged = accumulated / scale_total[..., None]
    return merged.reshape(micro_count, all_rows, row_width).astype(jnp.bfloat16)
```

```python
import functools
import math

import jax
import jax.numpy as jnp
from jax import lax
from jax.experimental import pallas as pl
from jax.experimental.pallas import tpu as pltpu
from jax.sharding import PartitionSpec as P

KV_HEADS = 2
HEAD_DIM = 128
LOW = -1e30
STAT_ROWS = 8

VMEM = pl.BlockSpec(memory_space=pltpu.VMEM)
SMEM = pl.BlockSpec(memory_space=pltpu.SMEM)


def digit_masks(shards):
    assert shards >= 16 and shards & (shards - 1) == 0 and shards.bit_length() % 2 == 1
    masks = [[1], [2]]
    unit = 4
    wide = []
    while unit < shards:
        wide.append([unit, 2 * unit, 3 * unit])
        unit *= 4
    return masks + wide[::-1]


def pairs(shards, mask):
    return [(i, i ^ mask) for i in range(shards)]


def split3(x):
    high = x.astype(jnp.bfloat16)
    rest = x - high.astype(jnp.float32)
    mid = rest.astype(jnp.bfloat16)
    low = (rest - mid.astype(jnp.float32)).astype(jnp.bfloat16)
    return [part.astype(jnp.float32) for part in (high, mid, low)]


def packed(num, peak, total):
    rows = split3(peak) + split3(total)
    rows.append(jnp.zeros((STAT_ROWS - len(rows), num.shape[1]), jnp.float32))
    return jnp.concatenate([num] + rows, axis=0).astype(jnp.bfloat16)


def unpacked(block):
    block = block.astype(jnp.float32)
    stats = block[HEAD_DIM:]
    peak = (stats[0:1] + stats[1:2]) + stats[2:3]
    total = (stats[3:4] + stats[4:5]) + stats[5:6]
    return block[:HEAD_DIM], peak, total


def kept(num, peak, total):
    pad = jnp.zeros((STAT_ROWS - 2, num.shape[1]), jnp.float32)
    return jnp.concatenate([num, peak, total, pad], axis=0)


def unkept(block):
    return block[:HEAD_DIM], block[HEAD_DIM : HEAD_DIM + 1], block[HEAD_DIM + 1 : HEAD_DIM + 2]


def merged(parts):
    peak = functools.reduce(jnp.maximum, [part[1] for part in parts])
    scales = [jnp.exp2(part[1] - peak) for part in parts]
    num = sum(part[0] * scale for part, scale in zip(parts, scales))
    total = sum(part[2] * scale for part, scale in zip(parts, scales))
    return num, peak, total


def transpose_kernel(v_ref, vt_ref):
    for micro in range(v_ref.shape[0]):
        vt_ref[micro] = v_ref[micro].T


def attend_kernel(local_rows, lane_masks, send, info_ref, len_ref, off_ref, q_ref, k_ref, vt_ref, out_ref):
    groups, lanes, _ = q_ref.shape
    key_count = k_ref.shape[1]
    me = info_ref[0]
    width = lanes // len(lane_masks)
    lane = lax.broadcasted_iota(jnp.int32, (1, lanes), 1)
    origin = jnp.full((1, lanes), lane_masks[0], jnp.int32)
    for index, mask in enumerate(lane_masks):
        origin = jnp.where(lane // width == index, mask, origin)
    row = (origin ^ me) * local_rows + lane % local_rows
    unit = math.log2(math.e) / math.sqrt(HEAD_DIM)
    key = lax.broadcasted_iota(jnp.int32, (key_count, lanes), 0)
    for group in range(groups):
        micro, head = divmod(group, KV_HEADS)
        last = jnp.minimum(off_ref[micro] + row, len_ref[micro] - 1) - me * key_count
        span = slice(head * HEAD_DIM, (head + 1) * HEAD_DIM)
        scores = lax.dot_general(
            k_ref[micro, :, span],
            q_ref[group],
            (((1,), (1,)), ((), ())),
            preferred_element_type=jnp.float32,
        )
        scores = jnp.where(key <= last, scores, LOW)
        top = jnp.max(scores, axis=0, keepdims=True)
        some = last >= 0
        top = jnp.where(some, top, 0.0)
        weights = jnp.exp2((scores - top) * unit)
        total = jnp.sum(weights, axis=0, keepdims=True)
        num = jnp.dot(
            vt_ref[micro, span, :], weights.astype(jnp.bfloat16), preferred_element_type=jnp.float32
        )
        peak = jnp.where(some, top * unit, LOW)
        out_ref[group] = packed(num, peak, total) if send else kept(num, peak, total)


def merge_kernel(ways, received, keep_ref, *refs):
    got_refs, own_ref, send_refs = refs[:received], refs[received], refs[received + 1 :]
    groups, _, lanes = keep_ref.shape
    width = lanes // ways
    for group in range(groups):
        parts = [unkept(keep_ref[group])] + [unpacked(got[group]) for got in got_refs]
        num, peak, total = merged(parts)
        for way in range(ways):
            span = slice(way * width, (way + 1) * width)
            part = (num[:, span], peak[:, span], total[:, span])
            if way == 0:
                own_ref[group] = kept(*part)
            else:
                send_refs[way - 1][group] = packed(*part)


def gather_lanes(blocks, way, width):
    lanes = blocks[0].shape[1]
    lane = lax.broadcasted_iota(jnp.int32, (1, lanes), 1) // width
    picked = None
    for group, block in enumerate(blocks):
        shift = (group - way) * width % lanes
        moved = pltpu.roll(block, shift, 1) if shift else block
        picked = moved if picked is None else jnp.where(lane == group, moved, picked)
    return picked


def merge_repack_kernel(ways, received, keep_ref, *refs):
    got_refs, own_ref, send_refs = refs[:received], refs[received], refs[received + 1 :]
    groups, _, lanes = keep_ref.shape
    width = lanes // ways
    done = []
    for group in range(groups):
        parts = [unkept(keep_ref[group])] + [unpacked(got[group]) for got in got_refs]
        done.append(kept(*merged(parts)))
    for way in range(ways):
        block = gather_lanes(done, way, width)
        if way == 0:
            own_ref[...] = block
        else:
            send_refs[way - 1][...] = packed(*unkept(block))


def final_kernel(keep_ref, *refs):
    got_refs, out_ref = refs[:-1], refs[-1]
    parts = [unkept(keep_ref[...])] + [unpacked(got[...]) for got in got_refs]
    num, _, total = merged(parts)
    out_ref[...] = (num / total).T.astype(jnp.bfloat16)


def call(kernel, outs, specs, flops=0, nbytes=0, grant=4):
    return pl.pallas_call(
        kernel,
        out_shape=outs,
        in_specs=specs,
        out_specs=jax.tree.map(lambda _: VMEM, outs),
        cost_estimate=pl.CostEstimate(flops=flops, bytes_accessed=nbytes, transcendentals=0),
        compiler_params=pltpu.CompilerParams(vmem_limit_bytes=grant << 20),
    )


def struct(shape, dtype):
    return jax.ShapeDtypeStruct(shape, dtype)


def body(queries, keys, values, lengths, offsets):
    micro_count, local_rows, row_width = queries.shape
    heads = row_width // HEAD_DIM
    share = heads // KV_HEADS
    groups = micro_count * KV_HEADS
    width = share * local_rows
    shards = lax.axis_size("blk")
    masks = digit_masks(shards)
    stacked = HEAD_DIM + STAT_ROWS
    info = jnp.reshape(lax.axis_index("blk"), (1,)).astype(jnp.int32)

    own = queries.reshape(micro_count, local_rows, KV_HEADS, share, HEAD_DIM)
    own = own.transpose(0, 2, 3, 1, 4).reshape(groups, width, HEAD_DIM)
    values_t = call(
        transpose_kernel, struct((micro_count, values.shape[2], values.shape[1]), values.dtype), [VMEM]
    )(values)

    origin = [0]
    piece = own
    for level in masks[:1:-1]:
        piece = jnp.concatenate(
            [piece] + [lax.ppermute(piece, "blk", pairs(shards, mask)) for mask in level], axis=1
        )
        origin = [base ^ mask for mask in [0] + level for base in origin]
    near = piece
    far = lax.ppermute(near, "blk", pairs(shards, 2))
    near_far = jnp.concatenate([near, far], axis=1)
    across = lax.ppermute(near_far, "blk", pairs(shards, 1))
    near_origin = origin + [base ^ 2 for base in origin]

    lanes = near_far.shape[1]

    def attend(rows, mask, send):
        return call(
            functools.partial(attend_kernel, local_rows, [base ^ mask for base in near_origin], send),
            struct((groups, stacked, lanes), jnp.bfloat16 if send else jnp.float32),
            [SMEM, SMEM, SMEM, VMEM, VMEM, VMEM],
            flops=4 * groups * lanes * keys.shape[1] * HEAD_DIM,
            grant=24,
        )(info, lengths, offsets, rows, keys, values_t)

    sends = attend(across, 1, True)
    got = [lax.ppermute(sends, "blk", pairs(shards, 1))]
    keep = attend(near_far, 0, False)
    for step in range(1, len(masks)):
        level = masks[step]
        ways = len(level) + 1
        if step < len(masks) - 1:
            kernel = merge_kernel
            shape = (groups, stacked, lanes // ways)
        else:
            kernel = merge_repack_kernel
            shape = (stacked, groups * width)
        lanes //= ways
        outs = [struct(shape, jnp.float32)] + [struct(shape, jnp.bfloat16)] * len(level)
        keep, *sends = call(
            functools.partial(kernel, ways, len(got)), outs, [VMEM] * (1 + len(got))
        )(keep, *got)
        got = [lax.ppermute(part, "blk", pairs(shards, mask)) for part, mask in zip(sends, level)]
    merged_rows = call(
        final_kernel, struct((groups * width, HEAD_DIM), jnp.bfloat16), [VMEM] * (1 + len(got))
    )(keep, *got)
    shaped = merged_rows.reshape(micro_count, KV_HEADS, share, local_rows, HEAD_DIM)
    return shaped.transpose(0, 3, 1, 2, 4).reshape(micro_count, local_rows, row_width)


def solution(mesh):
    return jax.shard_map(
        body,
        mesh=mesh,
        in_specs=(
            P("group", "blk", None),
            P("group", "blk", None),
            P("group", "blk", None),
            P("group"),
            P("group"),
        ),
        out_specs=P("group", "blk", None),
        check_vma=False,
    )
```

```python
import functools
import math

import jax
import jax.numpy as jnp
from jax import lax
from jax.experimental import pallas as pl
from jax.experimental.pallas import tpu as pltpu
from jax.sharding import PartitionSpec as P

KV_HEADS = 2
HEAD_DIM = 128
LOW = -1e30
STAT_ROWS = 8
PARTS = 5

VMEM = pl.BlockSpec(memory_space=pltpu.VMEM)
HBM = pl.BlockSpec(memory_space=pltpu.HBM)
SMEM = pl.BlockSpec(memory_space=pltpu.SMEM)


def digit_masks(shards):
    assert shards >= 16 and shards & (shards - 1) == 0 and shards.bit_length() % 2 == 1
    masks = [[1], [2]]
    unit = 4
    wide = []
    while unit < shards:
        wide.append([unit, 2 * unit, 3 * unit])
        unit *= 4
    return masks + wide[::-1]


def pairs(shards, mask):
    return [(i, i ^ mask) for i in range(shards)]


def split3(x):
    high = x.astype(jnp.bfloat16)
    rest = x - high.astype(jnp.float32)
    mid = rest.astype(jnp.bfloat16)
    low = (rest - mid.astype(jnp.float32)).astype(jnp.bfloat16)
    return [part.astype(jnp.float32) for part in (high, mid, low)]


def packed(num, peak, total):
    rows = split3(peak) + split3(total)
    rows.append(jnp.zeros((STAT_ROWS - len(rows), num.shape[1]), jnp.float32))
    return jnp.concatenate([num] + rows, axis=0).astype(jnp.bfloat16)


def unpacked(block):
    block = block.astype(jnp.float32)
    stats = block[HEAD_DIM:]
    peak = (stats[0:1] + stats[1:2]) + stats[2:3]
    total = (stats[3:4] + stats[4:5]) + stats[5:6]
    return block[:HEAD_DIM], peak, total


def kept(num, peak, total):
    pad = jnp.zeros((STAT_ROWS - 2, num.shape[1]), jnp.float32)
    return jnp.concatenate([num, peak, total, pad], axis=0)


def unkept(block):
    return block[:HEAD_DIM], block[HEAD_DIM : HEAD_DIM + 1], block[HEAD_DIM + 1 : HEAD_DIM + 2]


def merged(parts):
    peak = functools.reduce(jnp.maximum, [part[1] for part in parts])
    scales = [jnp.exp2(part[1] - peak) for part in parts]
    num = sum(part[0] * scale for part, scale in zip(parts, scales))
    total = sum(part[2] * scale for part, scale in zip(parts, scales))
    return num, peak, total


def prep_kernel(info_ref, len_hbm, off_hbm, q_hbm, k_hbm, v_hbm, q_ref, k_ref, vt_ref, mask_ref, v_ref, len_ref, off_ref, sem):
    micros, key_count, rows = mask_ref.shape
    chunk = key_count // PARTS

    def copies(source, target, first):
        made = []
        for micro in range(micros):
            for part in range(PARTS):
                cut = pl.ds(part * chunk, chunk)
                made.append(
                    pltpu.make_async_copy(
                        source.at[micro, cut], target.at[micro, cut], sem.at[first + len(made)]
                    )
                )
        return made

    own = pltpu.make_async_copy(q_hbm, q_ref, sem.at[2 * micros * PARTS])
    value_copies = copies(v_hbm, v_ref, 0)
    key_copies = copies(k_hbm, k_ref, micros * PARTS)
    bounds = [
        pltpu.make_async_copy(len_hbm, len_ref, sem.at[2 * micros * PARTS + 1]),
        pltpu.make_async_copy(off_hbm, off_ref, sem.at[2 * micros * PARTS + 2]),
    ]
    for copy in bounds + value_copies + [own] + key_copies:
        copy.start()
    for copy in bounds:
        copy.wait()
    first = info_ref[0] * key_count
    row = lax.broadcasted_iota(jnp.int32, (1, rows), 1)
    key = lax.broadcasted_iota(jnp.int32, (key_count, rows), 0)
    for micro in range(micros):
        last = jnp.minimum(off_ref[micro] + row, len_ref[micro] - 1) - first
        mask_ref[micro] = jnp.where(key <= last, 0.0, LOW).astype(mask_ref.dtype)
        for head in range(KV_HEADS):
            vt_ref[micro * KV_HEADS + head, HEAD_DIM:] = jnp.ones((STAT_ROWS, key_count), vt_ref.dtype)
    for micro in range(micros):
        for part in range(PARTS):
            cut = slice(part * chunk, (part + 1) * chunk)
            value_copies[micro * PARTS + part].wait()
            for head in range(KV_HEADS):
                span = slice(head * HEAD_DIM, (head + 1) * HEAD_DIM)
                vt_ref[micro * KV_HEADS + head, :HEAD_DIM, cut] = v_ref[micro, cut, span].T
    for copy in [own] + key_copies:
        copy.wait()


def attend_kernel(local_rows, masks, sends, info_ref, *refs):
    count = len(sends)
    q_refs, (k_ref, vt_ref, mask_ref), refs = refs[:count], refs[count : count + 3], refs[count + 3 :]
    out_refs, s_ref = refs[:count], refs[count]
    groups = q_refs[0].shape[0]
    block = q_refs[0].shape[1]
    lanes = block * count
    table = mask_ref.shape[2]
    me = info_ref[0]
    width = lanes // len(masks)
    lane = lax.broadcasted_iota(jnp.int32, (lanes, table), 0)
    origin = jnp.full((lanes, table), masks[0], jnp.int32)
    for index, mask in enumerate(masks):
        origin = jnp.where(lane // width == index, mask, origin)
    row = (origin ^ me) * local_rows + lane % local_rows
    chosen = (row == lax.broadcasted_iota(jnp.int32, (lanes, table), 1)).astype(jnp.float32)
    chosen = chosen.astype(k_ref.dtype)
    unit = math.log2(math.e) / math.sqrt(HEAD_DIM)

    def score(group):
        micro, head = divmod(group, KV_HEADS)
        span = slice(head * HEAD_DIM, (head + 1) * HEAD_DIM)
        rows = jnp.concatenate([ref[group] for ref in q_refs], axis=0)
        scores = lax.dot_general(
            jnp.concatenate([k_ref[micro, :, span], mask_ref[micro]], axis=1),
            jnp.concatenate([rows, chosen], axis=1),
            (((1,), (1,)), ((), ())),
            preferred_element_type=jnp.float32,
        )
        s_ref[group % 2] = scores
        return jnp.max(scores, axis=0, keepdims=True)

    def weigh(group, top):
        some = top > LOW / 2
        top = jnp.where(some, top, 0.0)
        weights = jnp.exp2((s_ref[group % 2] - top) * unit)
        num = jnp.dot(vt_ref[group], weights.astype(vt_ref.dtype), preferred_element_type=jnp.float32)
        total = num[HEAD_DIM : HEAD_DIM + 1]
        peak = jnp.where(some, top * unit, LOW)
        for index, send in enumerate(sends):
            cut = slice(index * block, (index + 1) * block)
            part = (num[:HEAD_DIM, cut], peak[:, cut], total[:, cut])
            out_refs[index][group] = packed(*part) if send else kept(*part)

    top = score(0)
    for group in range(groups):
        following = score(group + 1) if group + 1 < groups else None
        weigh(group, top)
        top = following


def merge_kernel(ways, received, keep_ref, *refs):
    got_refs, own_ref, send_refs = refs[:received], refs[received], refs[received + 1 :]
    groups, _, lanes = keep_ref.shape
    width = lanes // ways
    for group in range(groups):
        parts = [unkept(keep_ref[group])] + [unpacked(got[group]) for got in got_refs]
        num, peak, total = merged(parts)
        for way in range(ways):
            span = slice(way * width, (way + 1) * width)
            part = (num[:, span], peak[:, span], total[:, span])
            if way == 0:
                own_ref[group] = kept(*part)
            else:
                send_refs[way - 1][group] = packed(*part)


def gather_lanes(blocks, way, width):
    lanes = blocks[0].shape[1]
    lane = lax.broadcasted_iota(jnp.int32, (1, lanes), 1) // width
    picked = None
    for group, block in enumerate(blocks):
        shift = (group - way) * width % lanes
        moved = pltpu.roll(block, shift, 1) if shift else block
        picked = moved if picked is None else jnp.where(lane == group, moved, picked)
    return picked


def merge_repack_kernel(ways, received, keep_ref, *refs):
    got_refs, own_ref, send_refs = refs[:received], refs[received], refs[received + 1 :]
    groups, _, lanes = keep_ref.shape
    width = lanes // ways
    done = []
    for group in range(groups):
        parts = [unkept(keep_ref[group])] + [unpacked(got[group]) for got in got_refs]
        done.append(kept(*merged(parts)))
    for way in range(ways):
        block = gather_lanes(done, way, width)
        if way == 0:
            own_ref[...] = block
        else:
            send_refs[way - 1][...] = packed(*unkept(block))


def join_kernel(send, keep_ref, got_ref, out_ref):
    for group in range(keep_ref.shape[0]):
        part = merged([unkept(keep_ref[group]), unpacked(got_ref[group])])
        out_ref[group] = packed(*part) if send else kept(*part)


def final_kernel(keep_ref, *refs):
    got_refs, out_ref = refs[:-1], refs[-1]
    parts = [unkept(keep_ref[...])] + [unpacked(got[...]) for got in got_refs]
    num, _, total = merged(parts)
    out_ref[...] = (num / total).T.astype(jnp.bfloat16)


def call(kernel, outs, specs, flops=0, nbytes=0, grant=4, scratch=()):
    return pl.pallas_call(
        kernel,
        out_shape=outs,
        in_specs=specs,
        out_specs=jax.tree.map(lambda _: VMEM, outs),
        scratch_shapes=list(scratch),
        cost_estimate=pl.CostEstimate(flops=flops, bytes_accessed=nbytes, transcendentals=0),
        compiler_params=pltpu.CompilerParams(vmem_limit_bytes=grant << 20),
    )


def in_hbm(part):
    return pltpu.with_memory_space_constraint(part, pltpu.HBM)


def struct(shape, dtype):
    return jax.ShapeDtypeStruct(shape, dtype)


def program(queries, keys, values, lengths, offsets):
    micro_count, local_rows, row_width = queries.shape
    heads = row_width // HEAD_DIM
    share = heads // KV_HEADS
    groups = micro_count * KV_HEADS
    width = share * local_rows
    shards = lax.axis_size("blk")
    key_count = keys.shape[1]
    masks = digit_masks(shards)
    stacked = HEAD_DIM + STAT_ROWS
    table = -(-shards * local_rows // HEAD_DIM) * HEAD_DIM
    info = jnp.reshape(lax.axis_index("blk"), (1,)).astype(jnp.int32)
    low = keys.dtype

    def swap(part, mask):
        return lax.ppermute(part, "blk", pairs(shards, mask))

    own = queries.reshape(micro_count, local_rows, KV_HEADS, share, HEAD_DIM)
    own = own.transpose(0, 2, 3, 1, 4).reshape(groups, width, HEAD_DIM)
    near, keys_in, values_t, seen = call(
        prep_kernel,
        [
            struct(own.shape, low),
            struct(keys.shape, low),
            struct((groups, stacked, key_count), low),
            struct((micro_count, key_count, table), low),
        ],
        [SMEM] + [HBM] * 5,
        nbytes=2 * keys.size * 2,
        grant=8,
        scratch=[pltpu.VMEM(values.shape, low), pltpu.SMEM(lengths.shape, jnp.int32), pltpu.SMEM(offsets.shape, jnp.int32), pltpu.SemaphoreType.DMA((2 * micro_count * PARTS + 3,))],
    )(info, *[in_hbm(part) for part in (lengths, offsets, own, keys, values)])

    origin = [0]
    source = own
    for level in masks[:1:-1]:
        got = [swap(source, mask) for mask in level]
        near = source = jnp.concatenate([near] + got, axis=1)
        origin = [base ^ mask for mask in [0] + level for base in origin]
    block = near.shape[1]

    def attend(rows, shifts, sends):
        count = len(rows)
        return call(
            functools.partial(attend_kernel, local_rows, [base ^ shift for shift in shifts for base in origin], sends),
            [struct((groups, stacked, block), low if send else jnp.float32) for send in sends],
            [SMEM] + [VMEM] * (count + 3),
            flops=6 * groups * block * count * key_count * HEAD_DIM,
            grant=16,
            scratch=[pltpu.VMEM((2, key_count, block * count), jnp.float32)],
        )(info, *rows, keys_in, values_t, seen)

    far = swap(near, 2)
    near_across = swap(near, 1)
    near_keep, near_send = attend([near, near_across], [0, 1], [False, True])
    near_got = swap(near_send, 1)
    far_across = swap(far, 1)
    far_keep, far_send = attend([far, far_across], [2, 3], [False, True])
    far_got = swap(far_send, 1)
    outgoing = call(
        functools.partial(join_kernel, True), struct((groups, stacked, block), low), [VMEM] * 2
    )(far_keep, far_got)
    got = [swap(outgoing, 2)]
    keep = call(
        functools.partial(join_kernel, False), struct((groups, stacked, block), jnp.float32), [VMEM] * 2
    )(near_keep, near_got)
    lanes = block
    for step in range(2, len(masks)):
        level = masks[step]
        ways = len(level) + 1
        if step < len(masks) - 1:
            kernel = merge_kernel
            shape = (groups, stacked, lanes // ways)
        else:
            kernel = merge_repack_kernel
            shape = (stacked, groups * width)
        lanes //= ways
        outs = [struct(shape, jnp.float32)] + [struct(shape, low)] * len(level)
        keep, *sends = call(
            functools.partial(kernel, ways, len(got)), outs, [VMEM] * (1 + len(got))
        )(keep, *got)
        got = [swap(part, mask) for part, mask in zip(sends, level)]
    merged_rows = call(
        final_kernel, struct((groups * width, HEAD_DIM), low), [VMEM] * (1 + len(got))
    )(keep, *got)
    shaped = merged_rows.reshape(micro_count, KV_HEADS, share, local_rows, HEAD_DIM)
    return shaped.transpose(0, 3, 1, 2, 4).reshape(micro_count, local_rows, row_width)


def solution(mesh):
    return jax.shard_map(
        program,
        mesh=mesh,
        in_specs=(
            P("group", "blk", None),
            P("group", "blk", None),
            P("group", "blk", None),
            P("group"),
            P("group"),
        ),
        out_specs=P("group", "blk", None),
        check_vma=False,
    )
```

```python
import functools
import math

import jax
import jax.numpy as jnp
from jax import lax
from jax.experimental import pallas as pl
from jax.experimental.pallas import tpu as pltpu
from jax.sharding import PartitionSpec as P

KV_HEADS = 2
HEAD_DIM = 128
LOW = -1e30
STAT_ROWS = 8
PARTS = 5

VMEM = pl.BlockSpec(memory_space=pltpu.VMEM)
HBM = pl.BlockSpec(memory_space=pltpu.HBM)
SMEM = pl.BlockSpec(memory_space=pltpu.SMEM)


def digit_masks(shards):
    assert shards >= 16 and shards & (shards - 1) == 0 and shards.bit_length() % 2 == 1
    masks = [[1], [2]]
    unit = 4
    wide = []
    while unit < shards:
        wide.append([unit, 2 * unit, 3 * unit])
        unit *= 4
    return masks + wide[::-1]


def pairs(shards, mask):
    return [(i, i ^ mask) for i in range(shards)]


def split3(x):
    high = x.astype(jnp.bfloat16)
    rest = x - high.astype(jnp.float32)
    mid = rest.astype(jnp.bfloat16)
    low = (rest - mid.astype(jnp.float32)).astype(jnp.bfloat16)
    return [part.astype(jnp.float32) for part in (high, mid, low)]


def packed(num, peak, total):
    rows = split3(peak) + split3(total)
    rows.append(jnp.zeros((STAT_ROWS - len(rows), num.shape[1]), jnp.float32))
    return jnp.concatenate([num] + rows, axis=0).astype(jnp.bfloat16)


def unpacked(block):
    block = block.astype(jnp.float32)
    stats = block[HEAD_DIM:]
    peak = (stats[0:1] + stats[1:2]) + stats[2:3]
    total = (stats[3:4] + stats[4:5]) + stats[5:6]
    return block[:HEAD_DIM], peak, total


def kept(num, peak, total):
    pad = jnp.zeros((STAT_ROWS - 2, num.shape[1]), jnp.float32)
    return jnp.concatenate([num, peak, total, pad], axis=0)


def unkept(block):
    return block[:HEAD_DIM], block[HEAD_DIM : HEAD_DIM + 1], block[HEAD_DIM + 1 : HEAD_DIM + 2]


def merged(parts):
    peak = functools.reduce(jnp.maximum, [part[1] for part in parts])
    scales = [jnp.exp2(part[1] - peak) for part in parts]
    num = sum(part[0] * scale for part, scale in zip(parts, scales))
    total = sum(part[2] * scale for part, scale in zip(parts, scales))
    return num, peak, total


def prep_kernel(info_ref, len_hbm, off_hbm, q_hbm, k_hbm, v_hbm, q_ref, k_ref, vt_ref, mask_ref, v_ref, len_ref, off_ref, sem):
    micros, key_count, rows = mask_ref.shape
    chunk = key_count // PARTS

    def copies(source, target, first):
        made = []
        for micro in range(micros):
            for part in range(PARTS):
                cut = pl.ds(part * chunk, chunk)
                made.append(
                    pltpu.make_async_copy(
                        source.at[micro, cut], target.at[micro, cut], sem.at[first + len(made)]
                    )
                )
        return made

    own = pltpu.make_async_copy(q_hbm, q_ref, sem.at[2 * micros * PARTS])
    value_copies = copies(v_hbm, v_ref, 0)
    key_copies = copies(k_hbm, k_ref, micros * PARTS)
    bounds = [
        pltpu.make_async_copy(len_hbm, len_ref, sem.at[2 * micros * PARTS + 1]),
        pltpu.make_async_copy(off_hbm, off_ref, sem.at[2 * micros * PARTS + 2]),
    ]
    for copy in bounds + value_copies + [own] + key_copies:
        copy.start()
    for copy in bounds:
        copy.wait()
    first = info_ref[0] * key_count
    row = lax.broadcasted_iota(jnp.int32, (1, rows), 1)
    key = lax.broadcasted_iota(jnp.int32, (key_count, rows), 0)
    for micro in range(micros):
        last = jnp.minimum(off_ref[micro] + row, len_ref[micro] - 1) - first
        mask_ref[micro] = jnp.where(key <= last, 0.0, LOW).astype(mask_ref.dtype)
        for head in range(KV_HEADS):
            vt_ref[micro * KV_HEADS + head, HEAD_DIM:] = jnp.ones((STAT_ROWS, key_count), vt_ref.dtype)
    for micro in range(micros):
        for part in range(PARTS):
            cut = slice(part * chunk, (part + 1) * chunk)
            value_copies[micro * PARTS + part].wait()
            for head in range(KV_HEADS):
                span = slice(head * HEAD_DIM, (head + 1) * HEAD_DIM)
                vt_ref[micro * KV_HEADS + head, :HEAD_DIM, cut] = v_ref[micro, cut, span].T
    for copy in [own] + key_copies:
        copy.wait()


def attend_kernel(local_rows, masks, sends, base, info_ref, *refs):
    count = len(sends)
    q_refs, (k_ref, vt_ref, mask_ref), refs = refs[:count], refs[count : count + 3], refs[count + 3 :]
    out_refs, s_ref = refs[:count], refs[count]
    groups = q_refs[0].shape[0]
    block = q_refs[0].shape[1]
    lanes = block * count
    table = mask_ref.shape[2]
    me = info_ref[0]
    width = lanes // len(masks)
    lane = lax.broadcasted_iota(jnp.int32, (lanes, table), 0)
    origin = jnp.full((lanes, table), masks[0], jnp.int32)
    for index, mask in enumerate(masks):
        origin = jnp.where(lane // width == index, mask, origin)
    row = (origin ^ me) * local_rows + lane % local_rows
    chosen = (row == lax.broadcasted_iota(jnp.int32, (lanes, table), 1)).astype(jnp.float32)
    chosen = chosen.astype(k_ref.dtype)
    unit = math.log2(math.e) / math.sqrt(HEAD_DIM)

    def score(group):
        micro, head = divmod(base + group, KV_HEADS)
        span = slice(head * HEAD_DIM, (head + 1) * HEAD_DIM)
        rows = jnp.concatenate([ref[group] for ref in q_refs], axis=0)
        scores = lax.dot_general(
            jnp.concatenate([k_ref[micro, :, span], mask_ref[micro]], axis=1),
            jnp.concatenate([rows, chosen], axis=1),
            (((1,), (1,)), ((), ())),
            preferred_element_type=jnp.float32,
        )
        s_ref[group % 2] = scores
        return jnp.max(scores, axis=0, keepdims=True)

    def weigh(group, top):
        some = top > LOW / 2
        top = jnp.where(some, top, 0.0)
        weights = jnp.exp2((s_ref[group % 2] - top) * unit)
        num = jnp.dot(vt_ref[base + group], weights.astype(vt_ref.dtype), preferred_element_type=jnp.float32)
        total = num[HEAD_DIM : HEAD_DIM + 1]
        peak = jnp.where(some, top * unit, LOW)
        for index, send in enumerate(sends):
            cut = slice(index * block, (index + 1) * block)
            part = (num[:HEAD_DIM, cut], peak[:, cut], total[:, cut])
            out_refs[index][group] = packed(*part) if send else kept(*part)

    top = score(0)
    for group in range(groups):
        following = score(group + 1) if group + 1 < groups else None
        weigh(group, top)
        top = following


def merge_kernel(ways, received, keep_ref, *refs):
    got_refs, own_ref, send_refs = refs[:received], refs[received], refs[received + 1 :]
    groups, _, lanes = keep_ref.shape
    width = lanes // ways
    for group in range(groups):
        parts = [unkept(keep_ref[group])] + [unpacked(got[group]) for got in got_refs]
        num, peak, total = merged(parts)
        for way in range(ways):
            span = slice(way * width, (way + 1) * width)
            part = (num[:, span], peak[:, span], total[:, span])
            if way == 0:
                own_ref[group] = kept(*part)
            else:
                send_refs[way - 1][group] = packed(*part)


def gather_lanes(blocks, way, width):
    lanes = blocks[0].shape[1]
    lane = lax.broadcasted_iota(jnp.int32, (1, lanes), 1) // width
    picked = None
    for group, block in enumerate(blocks):
        shift = (group - way) * width % lanes
        moved = pltpu.roll(block, shift, 1) if shift else block
        picked = moved if picked is None else jnp.where(lane == group, moved, picked)
    return picked


def merge_repack_kernel(ways, received, keep_ref, *refs):
    got_refs, own_ref, send_refs = refs[:received], refs[received], refs[received + 1 :]
    groups, _, lanes = keep_ref.shape
    width = lanes // ways
    done = []
    for group in range(groups):
        parts = [unkept(keep_ref[group])] + [unpacked(got[group]) for got in got_refs]
        done.append(kept(*merged(parts)))
    for way in range(ways):
        block = gather_lanes(done, way, width)
        if way == 0:
            own_ref[...] = block
        else:
            send_refs[way - 1][...] = packed(*unkept(block))


def join_kernel(send, keep_ref, got_ref, out_ref):
    for group in range(keep_ref.shape[0]):
        part = merged([unkept(keep_ref[group]), unpacked(got_ref[group])])
        out_ref[group] = packed(*part) if send else kept(*part)


def final_kernel(keep_ref, *refs):
    got_refs, out_ref = refs[:-1], refs[-1]
    parts = [unkept(keep_ref[...])] + [unpacked(got[...]) for got in got_refs]
    num, _, total = merged(parts)
    out_ref[...] = (num / total).T.astype(jnp.bfloat16)


def call(kernel, outs, specs, flops=0, nbytes=0, grant=4, scratch=()):
    return pl.pallas_call(
        kernel,
        out_shape=outs,
        in_specs=specs,
        out_specs=jax.tree.map(lambda _: VMEM, outs),
        scratch_shapes=list(scratch),
        cost_estimate=pl.CostEstimate(flops=flops, bytes_accessed=nbytes, transcendentals=0),
        compiler_params=pltpu.CompilerParams(vmem_limit_bytes=grant << 20),
    )


def in_hbm(part):
    return pltpu.with_memory_space_constraint(part, pltpu.HBM)


def struct(shape, dtype):
    return jax.ShapeDtypeStruct(shape, dtype)


def program(queries, keys, values, lengths, offsets):
    micro_count, local_rows, row_width = queries.shape
    heads = row_width // HEAD_DIM
    share = heads // KV_HEADS
    groups = micro_count * KV_HEADS
    width = share * local_rows
    shards = lax.axis_size("blk")
    key_count = keys.shape[1]
    masks = digit_masks(shards)
    stacked = HEAD_DIM + STAT_ROWS
    table = -(-shards * local_rows // HEAD_DIM) * HEAD_DIM
    info = jnp.reshape(lax.axis_index("blk"), (1,)).astype(jnp.int32)
    low = keys.dtype

    def swap(part, mask):
        return lax.ppermute(part, "blk", pairs(shards, mask))

    own = queries.reshape(micro_count, local_rows, KV_HEADS, share, HEAD_DIM)
    own = own.transpose(0, 2, 3, 1, 4).reshape(groups, width, HEAD_DIM)
    near, keys_in, values_t, seen = call(
        prep_kernel,
        [
            struct(own.shape, low),
            struct(keys.shape, low),
            struct((groups, stacked, key_count), low),
            struct((micro_count, key_count, table), low),
        ],
        [SMEM] + [HBM] * 5,
        nbytes=2 * keys.size * 2,
        grant=8,
        scratch=[pltpu.VMEM(values.shape, low), pltpu.SMEM(lengths.shape, jnp.int32), pltpu.SMEM(offsets.shape, jnp.int32), pltpu.SemaphoreType.DMA((2 * micro_count * PARTS + 3,))],
    )(info, *[in_hbm(part) for part in (lengths, offsets, own, keys, values)])

    origin = [0]
    source = own
    for level in masks[:1:-1]:
        got = [swap(source, mask) for mask in level]
        near = source = jnp.concatenate([near] + got, axis=1)
        origin = [base ^ mask for mask in [0] + level for base in origin]
    block = near.shape[1]

    def attend(rows, shifts, sends, base=0):
        count, held = len(rows), rows[0].shape[0]
        return call(
            functools.partial(
                attend_kernel,
                local_rows,
                [mask ^ shift for shift in shifts for mask in origin],
                sends,
                base,
            ),
            [struct((held, stacked, block), low if send else jnp.float32) for send in sends],
            [SMEM] + [VMEM] * (count + 3),
            flops=6 * held * block * count * key_count * HEAD_DIM,
            grant=16,
            scratch=[pltpu.VMEM((2, key_count, block * count), jnp.float32)],
        )(info, *rows, keys_in, values_t, seen)

    def join(send, keep, got):
        outs = struct(keep.shape, low if send else jnp.float32)
        return call(functools.partial(join_kernel, send), outs, [VMEM] * 2)(keep, got)

    micros = range(micro_count)
    near_across = swap(near, 1)
    fars = [swap(near[m * KV_HEADS : (m + 1) * KV_HEADS], 2) for m in micros]
    near_keep, near_send = attend([near, near_across], [0, 1], [False, True])
    near_got = swap(near_send, 1)
    got = []
    for m in micros:
        across = swap(fars[m], 1)
        far_keep, far_send = attend([fars[m], across], [2, 3], [False, True], m * KV_HEADS)
        far_got = swap(far_send, 1)
        got.append(swap(join(True, far_keep, far_got), 2))
    got = [jnp.concatenate(got, axis=0)]
    keep = join(False, near_keep, near_got)
    lanes = block
    for step in range(2, len(masks)):
        level = masks[step]
        ways = len(level) + 1
        if step < len(masks) - 1:
            kernel = merge_kernel
            shape = (groups, stacked, lanes // ways)
        else:
            kernel = merge_repack_kernel
            shape = (stacked, groups * width)
        lanes //= ways
        outs = [struct(shape, jnp.float32)] + [struct(shape, low)] * len(level)
        keep, *sends = call(
            functools.partial(kernel, ways, len(got)), outs, [VMEM] * (1 + len(got))
        )(keep, *got)
        got = [swap(part, mask) for part, mask in zip(sends, level)]
    merged_rows = call(
        final_kernel, struct((groups * width, HEAD_DIM), low), [VMEM] * (1 + len(got))
    )(keep, *got)
    shaped = merged_rows.reshape(micro_count, KV_HEADS, share, local_rows, HEAD_DIM)
    return shaped.transpose(0, 3, 1, 2, 4).reshape(micro_count, local_rows, row_width)


def solution(mesh):
    return jax.shard_map(
        program,
        mesh=mesh,
        in_specs=(
            P("group", "blk", None),
            P("group", "blk", None),
            P("group", "blk", None),
            P("group"),
            P("group"),
        ),
        out_specs=P("group", "blk", None),
        check_vma=False,
    )
```

```python
import functools
import math

import jax
import jax.numpy as jnp
from jax import lax
from jax.experimental import pallas as pl
from jax.experimental.pallas import tpu as pltpu
from jax.sharding import PartitionSpec as P

KV_HEADS = 2
HEAD_DIM = 128
LOW = -1e30
STAT_ROWS = 8
PARTS = 2
CHAINS = 16
FAR_PARTS = 2

VMEM = pl.BlockSpec(memory_space=pltpu.VMEM)
HBM = pl.BlockSpec(memory_space=pltpu.HBM)
SMEM = pl.BlockSpec(memory_space=pltpu.SMEM)


def digit_masks(shards):
    assert shards >= 16 and shards & (shards - 1) == 0 and shards.bit_length() % 2 == 1
    masks = [[1], [2]]
    unit = 4
    wide = []
    while unit < shards:
        one, two = unit, 2 * unit + 1
        wide.append([one, two, one ^ two])
        unit *= 4
    return masks + wide[::-1]


def pairs(shards, mask):
    return [(i, i ^ mask) for i in range(shards)]


def split3(x):
    high = x.astype(jnp.bfloat16)
    rest = x - high.astype(jnp.float32)
    mid = rest.astype(jnp.bfloat16)
    low = (rest - mid.astype(jnp.float32)).astype(jnp.bfloat16)
    return [part.astype(jnp.float32) for part in (high, mid, low)]


def packed(num, peak, total):
    rows = split3(peak) + split3(total)
    rows.append(jnp.zeros((STAT_ROWS - len(rows), num.shape[1]), jnp.float32))
    return jnp.concatenate([num] + rows, axis=0).astype(jnp.bfloat16)


def unpacked(block):
    block = block.astype(jnp.float32)
    stats = block[HEAD_DIM:]
    peak = (stats[0:1] + stats[1:2]) + stats[2:3]
    total = (stats[3:4] + stats[4:5]) + stats[5:6]
    return block[:HEAD_DIM], peak, total


def kept(num, peak, total):
    pad = jnp.zeros((STAT_ROWS - 2, num.shape[1]), jnp.float32)
    return jnp.concatenate([num, peak, total, pad], axis=0)


def unkept(block):
    return block[:HEAD_DIM], block[HEAD_DIM : HEAD_DIM + 1], block[HEAD_DIM + 1 : HEAD_DIM + 2]


def merged(parts):
    peak = functools.reduce(jnp.maximum, [part[1] for part in parts])
    scales = [jnp.exp2(part[1] - peak) for part in parts]
    num = sum(part[0] * scale for part, scale in zip(parts, scales))
    total = sum(part[2] * scale for part, scale in zip(parts, scales))
    return num, peak, total


def prep_kernel(local_rows, origins, info_ref, len_hbm, off_hbm, q_hbm, k_hbm, v_hbm, q_ref, k_ref, vt_ref, mask_ref, near_ref, far_ref, v_ref, len_ref, off_ref, sem):
    micros, key_count, rows = mask_ref.shape
    chunk = key_count // PARTS

    def copies(source, target, first):
        made = []
        for micro in range(micros):
            for part in range(PARTS):
                cut = pl.ds(part * chunk, chunk)
                made.append(
                    pltpu.make_async_copy(
                        source.at[micro, cut], target.at[micro, cut], sem.at[first + len(made)]
                    )
                )
        return made

    own = pltpu.make_async_copy(q_hbm, q_ref, sem.at[2 * micros * PARTS])
    value_copies = copies(v_hbm, v_ref, 0)
    key_copies = copies(k_hbm, k_ref, micros * PARTS)
    bounds = [
        pltpu.make_async_copy(len_hbm, len_ref, sem.at[2 * micros * PARTS + 1]),
        pltpu.make_async_copy(off_hbm, off_ref, sem.at[2 * micros * PARTS + 2]),
    ]
    for copy in bounds + value_copies + [own] + key_copies:
        copy.start()
    for copy in bounds:
        copy.wait()
    first = info_ref[0] * key_count
    row = lax.broadcasted_iota(jnp.int32, (1, rows), 1)
    key = lax.broadcasted_iota(jnp.int32, (key_count, rows), 0)
    for micro in range(micros):
        last = jnp.minimum(off_ref[micro] + row, len_ref[micro] - 1) - first
        mask_ref[micro] = jnp.where(key <= last, 0.0, LOW).astype(mask_ref.dtype)
        for head in range(KV_HEADS):
            vt_ref[micro * KV_HEADS + head, HEAD_DIM:] = jnp.ones((STAT_ROWS, key_count), vt_ref.dtype)
    for chosen_ref, masks in zip((near_ref, far_ref), origins):
        shape = chosen_ref.shape
        lane = lax.broadcasted_iota(jnp.int32, (shape[0], 1), 0)
        width = shape[0] // len(masks)
        origin = jnp.full((shape[0], 1), masks[0], jnp.int32)
        for index, mask in enumerate(masks):
            origin = jnp.where(lane // width == index, mask, origin)
        place = (origin ^ info_ref[0]) * local_rows + lane % local_rows
        same = place == lax.broadcasted_iota(jnp.int32, shape, 1)
        chosen_ref[...] = same.astype(jnp.float32).astype(chosen_ref.dtype)
    for micro in range(micros):
        for part in range(PARTS):
            cut = slice(part * chunk, (part + 1) * chunk)
            value_copies[micro * PARTS + part].wait()
            for head in range(KV_HEADS):
                span = slice(head * HEAD_DIM, (head + 1) * HEAD_DIM)
                vt_ref[micro * KV_HEADS + head, :HEAD_DIM, cut] = v_ref[micro, cut, span].T
    for copy in [own] + key_copies:
        copy.wait()


def attend_kernel(sends, base, info_ref, *refs):
    count = len(sends)
    q_refs, refs = refs[:count], refs[count:]
    k_ref, vt_ref, mask_ref, chosen_ref, *refs = refs
    out_refs, (s_ref, top_ref) = refs[:count], refs[count:]
    groups, block = out_refs[0].shape[0], q_refs[0].shape[1]
    lanes = block * count
    unit = math.log2(math.e) / math.sqrt(HEAD_DIM)

    def score(group):
        micro, head = divmod(base + group, KV_HEADS)
        span = slice(head * HEAD_DIM, (head + 1) * HEAD_DIM)
        rows = jnp.concatenate([ref[group] for ref in q_refs], axis=0)
        scores = lax.dot_general(
            jnp.concatenate([k_ref[micro, :, span], mask_ref[micro]], axis=1),
            jnp.concatenate([rows, chosen_ref[...]], axis=1),
            (((1,), (1,)), ((), ())),
            preferred_element_type=jnp.float32,
        )
        s_ref[group % 2] = scores
        top_ref[group % 2] = jnp.max(scores.reshape(-1, CHAINS, lanes), axis=0)

    def weigh(group):
        top = jnp.max(top_ref[group % 2], axis=0, keepdims=True)
        some = top > LOW / 2
        top = jnp.where(some, top, 0.0)
        weights = jnp.exp2((s_ref[group % 2] - top) * unit)
        num = jnp.dot(
            vt_ref[base + group], weights.astype(vt_ref.dtype), preferred_element_type=jnp.float32
        )
        total = num[HEAD_DIM : HEAD_DIM + 1]
        peak = jnp.where(some, top * unit, LOW)
        for index, send in enumerate(sends):
            cut = slice(index * block, (index + 1) * block)
            part = (num[:HEAD_DIM, cut], peak[:, cut], total[:, cut])
            out_refs[index][group] = packed(*part) if send else kept(*part)

    score(0)
    for group in range(groups):

        @pl.when(info_ref[0] >= 0)
        def _(group=group):
            if group + 1 < groups:
                score(group + 1)
            weigh(group)


def merge_kernel(ways, received, keep_ref, *refs):
    got_refs, own_ref, send_refs = refs[:received], refs[received], refs[received + 1 :]
    groups, _, lanes = keep_ref.shape
    width = lanes // ways
    for group in range(groups):
        parts = [unkept(keep_ref[group])] + [unpacked(got[group]) for got in got_refs]
        num, peak, total = merged(parts)
        for way in range(ways):
            span = slice(way * width, (way + 1) * width)
            part = (num[:, span], peak[:, span], total[:, span])
            if way == 0:
                own_ref[group] = kept(*part)
            else:
                send_refs[way - 1][group] = packed(*part)


def gather_lanes(blocks, way, width):
    lanes = blocks[0].shape[1]
    lane = lax.broadcasted_iota(jnp.int32, (1, lanes), 1) // width
    picked = None
    for group, block in enumerate(blocks):
        shift = (group - way) * width % lanes
        moved = pltpu.roll(block, shift, 1) if shift else block
        picked = moved if picked is None else jnp.where(lane == group, moved, picked)
    return picked


def merge_repack_kernel(ways, received, keep_ref, *refs):
    got_refs, own_ref, send_refs = refs[:received], refs[received], refs[received + 1 :]
    groups, _, lanes = keep_ref.shape
    width = lanes // ways
    done = []
    for group in range(groups):
        parts = [unkept(keep_ref[group])] + [unpacked(got[group]) for got in got_refs]
        done.append(kept(*merged(parts)))
    for way in range(ways):
        block = gather_lanes(done, way, width)
        if way == 0:
            own_ref[...] = block
        else:
            send_refs[way - 1][...] = packed(*unkept(block))


def join_kernel(send, keep_ref, got_ref, out_ref):
    for group in range(keep_ref.shape[0]):
        part = merged([unkept(keep_ref[group]), unpacked(got_ref[group])])
        out_ref[group] = packed(*part) if send else kept(*part)


def final_kernel(keep_ref, *refs):
    got_refs, out_ref = refs[:-1], refs[-1]
    parts = [unkept(keep_ref[...])] + [unpacked(got[...]) for got in got_refs]
    num, _, total = merged(parts)
    out_ref[...] = (num / total).T.astype(jnp.bfloat16)


def call(kernel, outs, specs, flops=0, nbytes=0, grant=4, scratch=()):
    return pl.pallas_call(
        kernel,
        out_shape=outs,
        in_specs=specs,
        out_specs=jax.tree.map(lambda _: VMEM, outs),
        scratch_shapes=list(scratch),
        cost_estimate=pl.CostEstimate(flops=flops, bytes_accessed=nbytes, transcendentals=0),
        compiler_params=pltpu.CompilerParams(vmem_limit_bytes=grant << 20),
    )


def in_hbm(part):
    return pltpu.with_memory_space_constraint(part, pltpu.HBM)


def struct(shape, dtype):
    return jax.ShapeDtypeStruct(shape, dtype)


def program(queries, keys, values, lengths, offsets):
    micro_count, local_rows, row_width = queries.shape
    heads = row_width // HEAD_DIM
    share = heads // KV_HEADS
    groups = micro_count * KV_HEADS
    width = share * local_rows
    shards = lax.axis_size("blk")
    key_count = keys.shape[1]
    masks = digit_masks(shards)
    beyond = masks[1][0]
    stacked = HEAD_DIM + STAT_ROWS
    table = -(-shards * local_rows // HEAD_DIM) * HEAD_DIM
    info = jnp.reshape(lax.axis_index("blk"), (1,)).astype(jnp.int32)
    low = keys.dtype

    def swap(part, mask):
        return lax.ppermute(part, "blk", pairs(shards, mask))

    own = queries.reshape(micro_count, local_rows, KV_HEADS, share, HEAD_DIM)
    own = own.transpose(0, 2, 3, 1, 4).reshape(groups, width, HEAD_DIM)
    origin = [0]
    for level in masks[:1:-1]:
        origin = [base ^ mask for mask in [0] + level for base in origin]
    block = len(origin) * width
    near_origin, far_origin = ([base ^ shift for shift in shifts for base in origin] for shifts in ((0, 1), (beyond, beyond ^ 1)))
    near, keys_in, values_t, seen, near_rows, far_rows = call(
        functools.partial(prep_kernel, local_rows, (near_origin, far_origin)),
        [
            struct(own.shape, low),
            struct(keys.shape, low),
            struct((groups, stacked, key_count), low),
            struct((micro_count, key_count, table), low),
            struct((2 * block, table), low),
            struct((2 * block, table), low),
        ],
        [SMEM] + [HBM] * 5,
        nbytes=2 * keys.size * 2,
        grant=8,
        scratch=[
            pltpu.VMEM(values.shape, low),
            pltpu.SMEM(lengths.shape, jnp.int32),
            pltpu.SMEM(offsets.shape, jnp.int32),
            pltpu.SemaphoreType.DMA((2 * micro_count * PARTS + 3,)),
        ],
    )(info, *[in_hbm(part) for part in (lengths, offsets, own, keys, values)])

    source = own
    for level in masks[:1:-1]:
        got = [swap(source, mask) for mask in level]
        near = source = jnp.concatenate([near] + got, axis=1)
    block = near.shape[1]

    def attend(rows, chosen, cut):
        count, held = len(rows), cut[1] - cut[0]
        return call(
            functools.partial(attend_kernel, [False, True], cut[0]),
            [struct((held, stacked, block), part) for part in (jnp.float32, low)],
            [SMEM] + [VMEM] * (count + 4),
            flops=6 * held * block * count * key_count * HEAD_DIM,
            grant=16,
            scratch=[
                pltpu.VMEM((2, key_count, block * count), jnp.float32),
                pltpu.VMEM((2, CHAINS, block * count), jnp.float32),
            ],
        )(info, *rows, keys_in, values_t, seen, chosen)

    def join(send, keep, got):
        outs = struct(keep.shape, low if send else jnp.float32)
        return call(functools.partial(join_kernel, send), outs, [VMEM] * 2)(keep, got)

    held = groups // FAR_PARTS
    cuts = [(p * held, (p + 1) * held) for p in range(FAR_PARTS)]
    near_across = swap(near, 1)
    fars = [swap(near[slice(*cut)], beyond) for cut in cuts]
    near_keep, near_send = attend([near, near_across], near_rows, (0, groups))
    near_got = swap(near_send, 1)
    got = []
    for p, cut in enumerate(cuts):
        across = swap(fars[p], 1)
        keep, send = attend([fars[p], across], far_rows, cut)
        keep = join(True, keep, swap(send, 1))
        got.append(swap(keep, beyond))
    got = [jnp.concatenate(got, axis=0)]
    keep = join(False, near_keep, near_got)
    lanes = block
    for step in range(2, len(masks)):
        level = masks[step]
        ways = len(level) + 1
        if step < len(masks) - 1:
            kernel = merge_kernel
            shape = (groups, stacked, lanes // ways)
        else:
            kernel = merge_repack_kernel
            shape = (stacked, groups * width)
        lanes //= ways
        outs = [struct(shape, jnp.float32)] + [struct(shape, low)] * len(level)
        keep, *sends = call(
            functools.partial(kernel, ways, len(got)), outs, [VMEM] * (1 + len(got))
        )(keep, *got)
        got = [swap(part, mask) for part, mask in zip(sends, level)]
    merged_rows = call(
        final_kernel, struct((groups * width, HEAD_DIM), low), [VMEM] * (1 + len(got))
    )(keep, *got)
    shaped = merged_rows.reshape(micro_count, KV_HEADS, share, local_rows, HEAD_DIM)
    return shaped.transpose(0, 3, 1, 2, 4).reshape(micro_count, local_rows, row_width)


def solution(mesh):
    return jax.shard_map(
        program,
        mesh=mesh,
        in_specs=(
            P("group", "blk", None),
            P("group", "blk", None),
            P("group", "blk", None),
            P("group"),
            P("group"),
        ),
        out_specs=P("group", "blk", None),
        check_vma=False,
    )
```

```python
import functools
import math

import jax
import jax.numpy as jnp
from jax import lax
from jax.experimental import pallas as pl
from jax.experimental.pallas import tpu as pltpu
from jax.sharding import PartitionSpec as P

KV_HEADS = 2
HEAD_DIM = 128
LOW = -1e30
STAT_ROWS = 8
PARTS = 2
CHAINS = 16
FAR_PARTS = 2

VMEM = pl.BlockSpec(memory_space=pltpu.VMEM)
HBM = pl.BlockSpec(memory_space=pltpu.HBM)
SMEM = pl.BlockSpec(memory_space=pltpu.SMEM)


def digit_masks(shards):
    assert shards >= 16 and shards & (shards - 1) == 0 and shards.bit_length() % 2 == 1
    masks = [[1], [2]]
    unit = 4
    wide = []
    while unit < shards:
        one, two = unit, 2 * unit + 1
        wide.append([one, two, one ^ two])
        unit *= 4
    return masks + wide[::-1]


def pairs(shards, mask):
    return [(i, i ^ mask) for i in range(shards)]


def split3(x):
    high = x.astype(jnp.bfloat16)
    rest = x - high.astype(jnp.float32)
    mid = rest.astype(jnp.bfloat16)
    low = (rest - mid.astype(jnp.float32)).astype(jnp.bfloat16)
    return [part.astype(jnp.float32) for part in (high, mid, low)]


def packed(num, peak, total):
    rows = split3(peak) + split3(total)
    rows.append(jnp.zeros((STAT_ROWS - len(rows), num.shape[1]), jnp.float32))
    return jnp.concatenate([num] + rows, axis=0).astype(jnp.bfloat16)


def unpacked(block):
    block = block.astype(jnp.float32)
    stats = block[HEAD_DIM:]
    peak = (stats[0:1] + stats[1:2]) + stats[2:3]
    total = (stats[3:4] + stats[4:5]) + stats[5:6]
    return block[:HEAD_DIM], peak, total


def kept(num, peak, total):
    pad = jnp.zeros((STAT_ROWS - 2, num.shape[1]), jnp.float32)
    return jnp.concatenate([num, peak, total, pad], axis=0)


def unkept(block):
    return block[:HEAD_DIM], block[HEAD_DIM : HEAD_DIM + 1], block[HEAD_DIM + 1 : HEAD_DIM + 2]


def merged(parts):
    peak = functools.reduce(jnp.maximum, [part[1] for part in parts])
    scales = [jnp.exp2(part[1] - peak) for part in parts]
    num = sum(part[0] * scale for part, scale in zip(parts, scales))
    total = sum(part[2] * scale for part, scale in zip(parts, scales))
    return num, peak, total


def prep_kernel(local_rows, origins, info_ref, len_hbm, off_hbm, q_hbm, k_hbm, v_hbm, q_ref, k_ref, vt_ref, mask_ref, near_ref, far_ref, v_ref, len_ref, off_ref, sem):
    micros, key_count, rows = mask_ref.shape
    chunk = key_count // PARTS

    def copies(source, target, first):
        made = []
        for micro in range(micros):
            for part in range(PARTS):
                cut = pl.ds(part * chunk, chunk)
                made.append(
                    pltpu.make_async_copy(
                        source.at[micro, cut], target.at[micro, cut], sem.at[first + len(made)]
                    )
                )
        return made

    own = pltpu.make_async_copy(q_hbm, q_ref, sem.at[2 * micros * PARTS])
    value_copies = copies(v_hbm, v_ref, 0)
    key_copies = copies(k_hbm, k_ref, micros * PARTS)
    bounds = [
        pltpu.make_async_copy(len_hbm, len_ref, sem.at[2 * micros * PARTS + 1]),
        pltpu.make_async_copy(off_hbm, off_ref, sem.at[2 * micros * PARTS + 2]),
    ]
    for copy in bounds + value_copies + [own] + key_copies:
        copy.start()
    for copy in bounds:
        copy.wait()
    first = info_ref[0] * key_count
    row = lax.broadcasted_iota(jnp.int32, (1, rows), 1)
    key = lax.broadcasted_iota(jnp.int32, (key_count, rows), 0)
    for micro in range(micros):
        last = jnp.minimum(off_ref[micro] + row, len_ref[micro] - 1) - first
        mask_ref[micro] = jnp.where(key <= last, 0.0, LOW).astype(mask_ref.dtype)
        for head in range(KV_HEADS):
            vt_ref[micro * KV_HEADS + head, HEAD_DIM:] = jnp.ones((STAT_ROWS, key_count), vt_ref.dtype)
    for chosen_ref, masks in zip((near_ref, far_ref), origins):
        shape = chosen_ref.shape
        lane = lax.broadcasted_iota(jnp.int32, (shape[0], 1), 0)
        width = shape[0] // len(masks)
        origin = jnp.full((shape[0], 1), masks[0], jnp.int32)
        for index, mask in enumerate(masks):
            origin = jnp.where(lane // width == index, mask, origin)
        place = (origin ^ info_ref[0]) * local_rows + lane % local_rows
        same = place == lax.broadcasted_iota(jnp.int32, shape, 1)
        chosen_ref[...] = same.astype(jnp.float32).astype(chosen_ref.dtype)
    for micro in range(micros):
        for part in range(PARTS):
            cut = slice(part * chunk, (part + 1) * chunk)
            value_copies[micro * PARTS + part].wait()
            for head in range(KV_HEADS):
                span = slice(head * HEAD_DIM, (head + 1) * HEAD_DIM)
                vt_ref[micro * KV_HEADS + head, :HEAD_DIM, cut] = v_ref[micro, cut, span].T
    for copy in [own] + key_copies:
        copy.wait()


def attend_kernel(sends, base, info_ref, *refs):
    count = len(sends)
    q_refs, refs = refs[:count], refs[count:]
    k_ref, vt_ref, mask_ref, chosen_ref, *refs = refs
    out_refs, (s_ref, top_ref) = refs[:count], refs[count:]
    groups, block = out_refs[0].shape[0], q_refs[0].shape[1]
    lanes = block * count
    unit = math.log2(math.e) / math.sqrt(HEAD_DIM)

    def score(group):
        micro, head = divmod(base + group, KV_HEADS)
        span = slice(head * HEAD_DIM, (head + 1) * HEAD_DIM)
        rows = jnp.concatenate([ref[group] for ref in q_refs], axis=0)
        scores = lax.dot_general(
            jnp.concatenate([k_ref[micro, :, span], mask_ref[micro]], axis=1),
            jnp.concatenate([rows, chosen_ref[...]], axis=1),
            (((1,), (1,)), ((), ())),
            preferred_element_type=jnp.float32,
        )
        s_ref[group % 2] = scores
        top_ref[group % 2] = jnp.max(scores.reshape(-1, CHAINS, lanes), axis=0)

    def weigh(group):
        top = jnp.max(top_ref[group % 2], axis=0, keepdims=True)
        some = top > LOW / 2
        top = jnp.where(some, top, 0.0)
        weights = jnp.exp2((s_ref[group % 2] - top) * unit)
        num = jnp.dot(
            vt_ref[base + group], weights.astype(vt_ref.dtype), preferred_element_type=jnp.float32
        )
        total = num[HEAD_DIM : HEAD_DIM + 1]
        peak = jnp.where(some, top * unit, LOW)
        for index, send in enumerate(sends):
            cut = slice(index * block, (index + 1) * block)
            part = (num[:HEAD_DIM, cut], peak[:, cut], total[:, cut])
            out_refs[index][group] = packed(*part) if send else kept(*part)

    score(0)
    for group in range(groups):

        @pl.when(info_ref[0] >= 0)
        def _(group=group):
            if group + 1 < groups:
                score(group + 1)
            weigh(group)


def merge_kernel(ways, received, keep_ref, *refs):
    got_refs, own_ref, send_refs = refs[:received], refs[received], refs[received + 1 :]
    groups, _, lanes = keep_ref.shape
    width = lanes // ways
    for group in range(groups):
        parts = [unkept(keep_ref[group])] + [unpacked(got[group]) for got in got_refs]
        num, peak, total = merged(parts)
        for way in range(ways):
            span = slice(way * width, (way + 1) * width)
            part = (num[:, span], peak[:, span], total[:, span])
            if way == 0:
                own_ref[group] = kept(*part)
            else:
                send_refs[way - 1][group] = packed(*part)


def gather_lanes(blocks, way, width):
    lanes = blocks[0].shape[1]
    lane = lax.broadcasted_iota(jnp.int32, (1, lanes), 1) // width
    picked = None
    for group, block in enumerate(blocks):
        shift = (group - way) * width % lanes
        moved = pltpu.roll(block, shift, 1) if shift else block
        picked = moved if picked is None else jnp.where(lane == group, moved, picked)
    return picked


def merge_repack_kernel(ways, received, keep_ref, *refs):
    got_refs, own_ref, send_refs = refs[:received], refs[received], refs[received + 1 :]
    groups, _, lanes = keep_ref.shape
    width = lanes // ways
    done = []
    for group in range(groups):
        parts = [unkept(keep_ref[group])] + [unpacked(got[group]) for got in got_refs]
        done.append(kept(*merged(parts)))
    for way in range(ways):
        block = gather_lanes(done, way, width)
        if way == 0:
            own_ref[...] = block
        else:
            send_refs[way - 1][...] = packed(*unkept(block))


def join_kernel(send, keep_ref, got_ref, out_ref):
    for group in range(keep_ref.shape[0]):
        part = merged([unkept(keep_ref[group]), unpacked(got_ref[group])])
        out_ref[group] = packed(*part) if send else kept(*part)


def final_kernel(keep_ref, *refs):
    got_refs, out_ref = refs[:-1], refs[-1]
    parts = [unkept(keep_ref[...])] + [unpacked(got[...]) for got in got_refs]
    num, _, total = merged(parts)
    out_ref[...] = (num / total).astype(jnp.bfloat16).T


def call(kernel, outs, specs, flops=0, nbytes=0, grant=4, scratch=()):
    return pl.pallas_call(
        kernel,
        out_shape=outs,
        in_specs=specs,
        out_specs=jax.tree.map(lambda _: VMEM, outs),
        scratch_shapes=list(scratch),
        cost_estimate=pl.CostEstimate(flops=flops, bytes_accessed=nbytes, transcendentals=0),
        compiler_params=pltpu.CompilerParams(vmem_limit_bytes=grant << 20),
    )


def in_hbm(part):
    return pltpu.with_memory_space_constraint(part, pltpu.HBM)


def struct(shape, dtype):
    return jax.ShapeDtypeStruct(shape, dtype)


def program(queries, keys, values, lengths, offsets):
    micro_count, local_rows, row_width = queries.shape
    heads = row_width // HEAD_DIM
    share = heads // KV_HEADS
    groups = micro_count * KV_HEADS
    width = share * local_rows
    shards = lax.axis_size("blk")
    key_count = keys.shape[1]
    masks = digit_masks(shards)
    beyond = masks[1][0]
    stacked = HEAD_DIM + STAT_ROWS
    table = -(-shards * local_rows // HEAD_DIM) * HEAD_DIM
    info = jnp.reshape(lax.axis_index("blk"), (1,)).astype(jnp.int32)
    low = keys.dtype

    def swap(part, mask):
        return lax.ppermute(part, "blk", pairs(shards, mask))

    own = queries.reshape(micro_count, local_rows, KV_HEADS, share, HEAD_DIM)
    own = own.transpose(0, 2, 3, 1, 4).reshape(groups, width, HEAD_DIM)
    origin = [0]
    for level in masks[:1:-1]:
        origin = [base ^ mask for mask in [0] + level for base in origin]
    block = len(origin) * width
    near_origin, far_origin = ([base ^ shift for shift in shifts for base in origin] for shifts in ((0, 1), (beyond, beyond ^ 1)))
    near, keys_in, values_t, seen, near_rows, far_rows = call(
        functools.partial(prep_kernel, local_rows, (near_origin, far_origin)),
        [
            struct(own.shape, low),
            struct(keys.shape, low),
            struct((groups, stacked, key_count), low),
            struct((micro_count, key_count, table), low),
            struct((2 * block, table), low),
            struct((2 * block, table), low),
        ],
        [SMEM] + [HBM] * 5,
        nbytes=2 * keys.size * 2,
        grant=8,
        scratch=[
            pltpu.VMEM(values.shape, low),
            pltpu.SMEM(lengths.shape, jnp.int32),
            pltpu.SMEM(offsets.shape, jnp.int32),
            pltpu.SemaphoreType.DMA((2 * micro_count * PARTS + 3,)),
        ],
    )(info, *[in_hbm(part) for part in (lengths, offsets, own, keys, values)])

    source = own
    for level in masks[:1:-1]:
        got = [swap(source, mask) for mask in level]
        near = source = jnp.concatenate([near] + got, axis=1)
    block = near.shape[1]

    def attend(rows, chosen, cut):
        count, held = len(rows), cut[1] - cut[0]
        return call(
            functools.partial(attend_kernel, [False, True], cut[0]),
            [struct((held, stacked, block), part) for part in (jnp.float32, low)],
            [SMEM] + [VMEM] * (count + 4),
            flops=6 * held * block * count * key_count * HEAD_DIM,
            grant=16,
            scratch=[
                pltpu.VMEM((2, key_count, block * count), jnp.float32),
                pltpu.VMEM((2, CHAINS, block * count), jnp.float32),
            ],
        )(info, *rows, keys_in, values_t, seen, chosen)

    def join(send, keep, got):
        outs = struct(keep.shape, low if send else jnp.float32)
        return call(functools.partial(join_kernel, send), outs, [VMEM] * 2)(keep, got)

    held = groups // FAR_PARTS
    cuts = [(p * held, (p + 1) * held) for p in range(FAR_PARTS)]
    near_across = swap(near, 1)
    fars = [swap(near[slice(*cut)], beyond) for cut in cuts]
    near_keep, near_send = attend([near, near_across], near_rows, (0, groups))
    near_got = swap(near_send, 1)
    got = []
    for p, cut in enumerate(cuts):
        across = swap(fars[p], 1)
        keep, send = attend([fars[p], across], far_rows, cut)
        keep = join(True, keep, swap(send, 1))
        got.append(swap(keep, beyond))
    got = [jnp.concatenate(got, axis=0)]
    keep = join(False, near_keep, near_got)
    lanes = block
    for step in range(2, len(masks)):
        level = masks[step]
        ways = len(level) + 1
        if step < len(masks) - 1:
            kernel = merge_kernel
            shape = (groups, stacked, lanes // ways)
        else:
            kernel = merge_repack_kernel
            shape = (stacked, groups * width)
        lanes //= ways
        outs = [struct(shape, jnp.float32)] + [struct(shape, low)] * len(level)
        keep, *sends = call(
            functools.partial(kernel, ways, len(got)), outs, [VMEM] * (1 + len(got))
        )(keep, *got)
        got = [swap(part, mask) for part, mask in zip(sends, level)]
    merged_rows = call(
        final_kernel, struct((groups * width, HEAD_DIM), low), [VMEM] * (1 + len(got))
    )(keep, *got)
    shaped = merged_rows.reshape(micro_count, KV_HEADS, share, local_rows, HEAD_DIM)
    return shaped.transpose(0, 3, 1, 2, 4).reshape(micro_count, local_rows, row_width)


def solution(mesh):
    return jax.shard_map(
        program,
        mesh=mesh,
        in_specs=(
            P("group", "blk", None),
            P("group", "blk", None),
            P("group", "blk", None),
            P("group"),
            P("group"),
        ),
        out_specs=P("group", "blk", None),
        check_vma=False,
    )
```
